32 devices in a mesh: row: 8 (over z, x), col: 4 (over y, core).
Axes of the slice: x: 2, y: 2, z: 4, core: 2. Of those that a mesh axis runs over, the one named last changes fastest.
Arguments:
- coeffs: float32 [4096, 4096], P('row', 'col'), may hold values from -6 to 6
- ham_alpha: float32 [4096, 4096], P('row'), may hold values from -1.5 to 7.5, as said below
- ham_beta: float32 [4096, 4096], P('col'), may hold values from -1.5 to 7.5, as said below
Outputs:
- sigma_vec: float32 [4096, 4096], P('row', 'col')
The draws below stay inside these ranges and needn't reach their ends.
Inputs may be any that keep to these rules, and one draw needn't show every extreme that they name: `ham_alpha`: symmetric. `ham_beta`: symmetric.
All inputs are finite; a program needn't handle non-finite values.
Results may differ from the reference program's by a relative error of at most 0.00005.
Values sent between devices are 32-bit elements; how exact they have to be, the bound alone decides.
A program may use at most 128 MiB of HBM per device.

```python
import jax
import jax.numpy as jnp
from jax import lax

NSTR = 4096


def make_hamiltonian(key, which):
    folded = jax.random.fold_in(key, which)
    key_off, key_diag = jax.random.split(folded)
    normals = jax.random.truncated_normal(key_off, -6.0, 6.0, (NSTR, NSTR), jnp.float32)
    symmetric = (normals + normals.T) / jnp.sqrt(2.0 * NSTR)
    diagonal = jax.random.uniform(key_diag, (NSTR,), jnp.float32, 1.0, 3.0)
    return symmetric + jnp.diag(diagonal)


def draw_ham_alpha(key, part):
    return make_hamiltonian(key, 11)


def draw_ham_beta(key, part):
    return make_hamiltonian(key, 23)


def levels(key, extent, pieces, low, high):
    factor_of, own = 1.0, jax.random.fold_in(key, 6)
    for dim, blocks in pieces:
        draws = jnp.exp(jax.random.uniform(jax.random.fold_in(own, dim), (blocks,), jnp.float32, low / len(pieces), high / len(pieces)))
        factor_of = factor_of * jnp.repeat(draws, extent[dim] // blocks).reshape([-1 if axis == dim else 1 for axis in range(len(extent))])
    return factor_of


def scatter_about(stream_key, shape, scale, bound, shards=(), held_as=jnp.bfloat16):
    factor_of = levels(stream_key, shape, shards, -0.22, 0.18) if shards else 1.0
    entries = jax.random.normal(stream_key, shape, jnp.float32) * scale * factor_of
    return jnp.minimum(jnp.maximum(entries, -bound), bound).astype(held_as)


def setup_inputs(seed: int = 0) -> dict:
    streams_of = jax.random.split(jax.random.key(seed), 4)
    coeffs = scatter_about(streams_of[0], (NSTR, NSTR), 1.0, 6.0, ((0, 8), (1, 4)), jnp.float32)
    ham_alpha = draw_ham_alpha(jax.random.fold_in(streams_of[3], 71), 0)
    ham_beta = draw_ham_beta(jax.random.fold_in(streams_of[3], 71), 0)
    return dict(coeffs=coeffs, ham_alpha=ham_alpha, ham_beta=ham_beta)


def reference(coeffs, ham_alpha, ham_beta):
    alpha_part = jnp.dot(ham_alpha, coeffs, precision=lax.Precision.HIGHEST, preferred_element_type=jnp.float32)
    beta_part = jnp.dot(coeffs, ham_beta.T, precision=lax.Precision.HIGHEST, preferred_element_type=jnp.float32)
    return alpha_part + beta_part
```

```python
import functools

import jax
import jax.numpy as jnp
from jax import lax
from jax.experimental import pallas as pl
from jax.experimental.pallas import tpu as pltpu
from jax.sharding import PartitionSpec as P

PAIR = 2
MESH = pl.DeviceIdType.MESH


def flip(index, key):
    bit = 1
    while bit <= key:
        if key & bit:
            index = index + bit - 2 * bit * ((index // bit) % 2)
        bit *= 2
    return index


def split(value):
    high = value.astype(jnp.bfloat16)
    return high, (value - high.astype(jnp.float32)).astype(jnp.bfloat16)


def product(lhs, rhs, rhs_dim):
    lhs_high, lhs_low = split(lhs)
    rhs_high, rhs_low = split(rhs)

    def one(a, b):
        return lax.dot_general(
            a, b, (((1,), (rhs_dim,)), ((), ())), preferred_element_type=jnp.float32
        )

    return one(lhs_high, rhs_high) + (one(lhs_high, rhs_low) + one(lhs_low, rhs_high))


def exchanges(n):
    held, mask, out = [0], n // 2, []
    while mask:
        out += [(mask, key) for key in held]
        held += [key ^ mask for key in held]
        mask //= 2
    return out


def kernel(
    line, cols_n, cw, width,
    coeffs, ha, hb, out,
    ham, beta, co, ag, sums, sums_in, acc, acc_in, turned, back_in,
    load_sem, ag_send, ag_recv, s_send, s_recv, o_send, o_recv,
    x_send, x_recv, p_send, p_recv, c_send, c_recv,
):
    rows, cols = coeffs.shape
    nk = cols // cw - 1
    row, col = lax.axis_index("row"), lax.axis_index("col")
    z, x = row // PAIR, row % PAIR
    partner = z * PAIR + 1 - x
    steps = exchanges(cols_n)
    masks = sorted({mask for mask, _ in steps}, reverse=True)

    def there(to_row, to_col):
        return (to_row, to_col)

    def ham_load(s):
        at = pl.multiple_of((s * PAIR + x) * rows, 128)
        return pltpu.make_async_copy(ha.at[:, pl.ds(at, rows)], ham.at[0, s], load_sem.at[s])

    def beta_load(key):
        at = pl.multiple_of(flip(col, key) * cols, 128)
        return pltpu.make_async_copy(
            hb.at[:, pl.ds(at, cols)], beta.at[key], load_sem.at[line + key]
        )

    beta_load(0).start()
    for s in range(line):
        ham_load(s).start()
    for key in range(1, cols_n):
        beta_load(key).start()

    barrier = pltpu.get_barrier_semaphore()
    has_low, has_high = z > 0, z < line - 1
    pl.semaphore_signal(barrier, inc=1, device_id=there(partner, col), device_id_type=MESH)
    for mask in masks:
        pl.semaphore_signal(
            barrier, inc=1, device_id=there(row, flip(col, mask)), device_id_type=MESH
        )

    @pl.when(has_low)
    def _():
        pl.semaphore_signal(barrier, inc=1, device_id=there(row - PAIR, col), device_id_type=MESH)

    @pl.when(has_high)
    def _():
        pl.semaphore_signal(barrier, inc=1, device_id=there(row + PAIR, col), device_id_type=MESH)

    inner = jnp.logical_and(has_low, has_high)

    @pl.when(inner)
    def _():
        pl.semaphore_wait(barrier, 3 + len(masks))

    @pl.when(jnp.logical_not(inner))
    def _():
        pl.semaphore_wait(barrier, 2 + len(masks))

    def remote(src, dst, send, recv, to):
        return pltpu.make_async_remote_copy(
            src_ref=src, dst_ref=dst, send_sem=send, recv_sem=recv,
            device_id=to, device_id_type=MESH,
        )

    def slot(index):
        first = index * width
        at = pl.multiple_of(first % rows, 128)
        return ham.at[1, first // rows, :, pl.ds(at, width)]

    def piece_copy():
        first = col * width
        at = pl.multiple_of((first // rows * PAIR + 1 - x) * rows + first % rows, 128)
        return remote(
            ha.at[:, pl.ds(at, width)], slot(col), x_send.at[0], x_recv.at[0], there(partner, col)
        )

    def back_copy():
        return remote(
            coeffs.at[:, pl.ds(nk * cw, cw)], back_in, x_send.at[1], x_recv.at[1],
            there(partner, col),
        )

    def other_copy(k):
        return remote(acc.at[1, k], acc_in.at[k], o_send.at[k], o_recv.at[k], there(partner, col))

    def ag_copy(d, t, k):
        src = coeffs.at[:, pl.ds(pl.multiple_of(k * cw, 128), cw)] if t == 1 else ag.at[d, t - 2, k]
        to = there(row + PAIR if d == 0 else row - PAIR, col)
        return remote(src, ag.at[d, t - 1, k], ag_send.at[d, t - 1, k], ag_recv.at[d, t - 1, k], to)

    def ag_sends(d, t):
        if d == 0:
            return jnp.logical_and(has_high, z >= t - 1)
        return jnp.logical_and(has_low, z <= line - t)

    def ag_gets(d, t):
        return z >= t if d == 0 else z <= line - 1 - t

    def s_copy(d, m):
        to = there(row + PAIR if d == 0 else row - PAIR, col)
        return remote(sums.at[d, m - 1], sums_in.at[d, m - 1], s_send.at[d, m - 1], s_recv.at[d, m - 1], to)

    def s_sends(d, m):
        return z <= line - 1 - m if d == 0 else z >= m

    def s_gets(d, m):
        if d == 0:
            return jnp.logical_and(z >= 1, z - 1 <= line - 1 - m)
        return jnp.logical_and(z <= line - 2, z + 1 >= m)

    def p_copy(i):
        mask, key = steps[i]
        place = slot(flip(col, key))
        return remote(place, place, p_send.at[i], p_recv.at[i], there(row, flip(col, mask)))

    def p_got(i):
        mask, key = steps[i]
        place = slot(flip(col, key ^ mask))
        return remote(place, place, p_send.at[i], p_recv.at[i], there(row, flip(col, mask)))

    half = rows // 2

    def c_copy(i, h):
        mask, key = steps[i]
        part = pl.ds(h * half, half)
        src = coeffs.at[part] if key == 0 else co.at[key - 1, part]
        return remote(
            src, co.at[(key ^ mask) - 1, part], c_send.at[i, h], c_recv.at[i, h],
            there(row, flip(col, mask)),
        )

    piece_copy().start()
    for d in range(2):
        @pl.when(ag_sends(d, 1))
        def _(d=d):
            for k in range(nk):
                ag_copy(d, 1, k).start()
    c_copy(0, 0).start()
    back_copy().start()

    tile = min(256, cols)

    def beta_tile(key_ref, beta_ref, n, add):
        at = pl.ds(pl.multiple_of(n * tile, 128), tile)
        value = product(key_ref[...], beta_ref[at, :], 1)
        out[:, at] = out[:, at] + value if add else value

    beta_load(0).wait()

    @pl.loop(0, cols // tile)
    def _(n):
        beta_tile(coeffs, beta.at[0], n, False)

    turned[0] = coeffs[:, nk * cw:].T
    for s in range(line):
        ham_load(s).wait()
    for key in range(1, cols_n):
        beta_load(key).wait()

    piece_copy().wait_recv()
    p_copy(0).start()
    c_copy(0, 1).start()

    def pass_on(t):
        for k in range(nk):
            for d in range(2):
                @pl.when(ag_gets(d, t))
                def _(d=d, k=k):
                    ag_copy(d, t, k).wait_recv()

                if t + 1 < line:
                    @pl.when(ag_sends(d, t + 1))
                    def _(d=d, k=k):
                        ag_copy(d, t + 1, k).start()

    pass_on(1)

    for mask in masks:
        group = [i for i, step in enumerate(steps) if step[0] == mask]
        for i in group:
            if i:
                p_copy(i).start()
        for i in group:
            p_got(i).wait_recv()
    back_copy().wait_recv()
    turned[1] = back_in[...].T

    def term(s):
        def body(m, total):
            return total + product(turned[m], ham[m, s], 0)

        return lax.fori_loop(0, PAIR, body, jnp.zeros((cw, rows), jnp.float32))

    def send_sums(m):
        for d in range(2):
            @pl.when(s_sends(d, m))
            def _(d=d):
                sums[d, m - 1] = term(z + m if d == 0 else z - m)

            if m + 1 < line:
                @pl.when(s_gets(d, m + 1))
                def _(d=d):
                    s_copy(d, m + 1).wait_recv()

                @pl.when(jnp.logical_and(s_gets(d, m + 1), s_sends(d, m)))
                def _(d=d):
                    sums[d, m - 1] = sums[d, m - 1] + sums_in[d, m]

            @pl.when(s_sends(d, m))
            def _(d=d):
                s_copy(d, m).start()

    def add_products(d, t, k):
        s = z - t if d == 0 else z + t

        @pl.loop(0, PAIR)
        def _(m):
            acc[m, k] = acc[m, k] + product(ham[m, s], ag[d, t - 1, k], 0)

    def add_step(t):
        for d in range(2):
            @pl.when(ag_gets(d, t))
            def _(d=d):
                @pl.loop(0, nk)
                def _(k):
                    add_products(d, t, k)

    if line > 1:
        send_sums(line - 1)

    @pl.loop(0, nk)
    def _(k):
        own = coeffs.at[:, pl.ds(pl.multiple_of(k * cw, 128), cw)]

        @pl.loop(0, PAIR)
        def _(m):
            acc[m, k] = product(ham[m, z], own[...], 0)

    def coeffs_step(mask):
        group = [i for i, step in enumerate(steps) if step[0] == mask]
        for i in group:
            if i:
                for h in range(2):
                    c_copy(i, h).start()
        for i in group:
            for h in range(2):
                c_copy(i, h).wait_recv()

    add_step(1)
    for t in range(2, line):
        if t < line - 1:
            pass_on(t)
        send_sums(line - t)
        if t == 2:
            coeffs_step(masks[0])
            if len(masks) > 1:
                for i, step in enumerate(steps):
                    if step[0] == masks[1]:
                        for h in range(2):
                            c_copy(i, h).start()
        if t < line - 1:
            add_step(t)

    for j, mask in enumerate(masks):
        group = [i for i, step in enumerate(steps) if step[0] == mask]
        if j >= 2:
            for i in group:
                for h in range(2):
                    c_copy(i, h).start()
        if j >= 1:
            for i in group:
                for h in range(2):
                    c_copy(i, h).wait_recv()

    @pl.loop(1, cols_n)
    def _(key):
        @pl.loop(0, cols // tile)
        def _(n):
            beta_tile(co.at[key - 1], beta.at[key], n, True)

    t = line - 1

    @pl.loop(0, nk)
    def _(k):
        for d in range(2):
            @pl.when(ag_gets(d, t))
            def _(d=d):
                ag_copy(d, t, k).wait_recv()
                add_products(d, t, k)

        other_copy(k).start()

    tail = term(z)
    for d in range(2):
        @pl.when(s_gets(d, 1))
        def _(d=d):
            s_copy(d, 1).wait_recv()
    sums[0, line - 1] = tail
    for d in range(2):
        @pl.when(s_gets(d, 1))
        def _(d=d):
            sums[0, line - 1] = sums[0, line - 1] + sums_in[d, 0]
    out[:, nk * cw:] = out[:, nk * cw:] + sums[0, line - 1].T

    @pl.loop(0, nk)
    def _(k):
        at = pl.ds(pl.multiple_of(k * cw, 128), cw)
        other_copy(k).wait_recv()
        out[:, at] = out[:, at] + (acc[0, k] + acc_in[k])

    piece_copy().wait_send()
    back_copy().wait_send()
    for i in range(len(steps)):
        p_copy(i).wait_send()
        for h in range(2):
            c_copy(i, h).wait_send()
    for d in range(2):
        for m in range(1, line):
            @pl.when(ag_sends(d, m))
            def _(d=d, m=m):
                for k in range(nk):
                    ag_copy(d, m, k).wait_send()

            @pl.when(s_sends(d, m))
            def _(d=d, m=m):
                s_copy(d, m).wait_send()

    @pl.loop(0, nk)
    def _(k):
        other_copy(k).wait_send()


def solution(mesh):
    line, cols_n = mesh.shape["row"] // PAIR, mesh.shape["col"]
    n_steps = len(exchanges(cols_n))

    def local(coeffs, ham_alpha, ham_beta):
        rows, cols = coeffs.shape
        cw = min(256, cols // 2)
        nk = cols // cw - 1
        width = line * rows // cols_n
        f32, dma = jnp.float32, pltpu.SemaphoreType.DMA
        any_spec = pl.BlockSpec(memory_space=pl.ANY)
        vmem_spec = pl.BlockSpec(memory_space=pltpu.VMEM)
        return pl.pallas_call(
            functools.partial(kernel, line, cols_n, cw, width),
            out_shape=jax.ShapeDtypeStruct((rows, cols), f32),
            in_specs=[vmem_spec, any_spec, any_spec],
            out_specs=vmem_spec,
            scratch_shapes=[
                pltpu.VMEM((PAIR, line, rows, rows), f32),
                pltpu.VMEM((cols_n, cols, cols), f32),
                pltpu.VMEM((cols_n - 1, rows, cols), f32),
                pltpu.VMEM((2, line - 1, nk, rows, cw), f32),
                pltpu.VMEM((2, line, cw, rows), f32),
                pltpu.VMEM((2, line - 1, cw, rows), f32),
                pltpu.VMEM((PAIR, nk, rows, cw), f32),
                pltpu.VMEM((nk, rows, cw), f32),
                pltpu.VMEM((PAIR, cw, rows), f32),
                pltpu.VMEM((rows, cw), f32),
                dma((line + cols_n,)),
                dma((2, line - 1, nk)),
                dma((2, line - 1, nk)),
                dma((2, line - 1)),
                dma((2, line - 1)),
                dma((nk,)),
                dma((nk,)),
                dma((2,)),
                dma((2,)),
                dma((n_steps,)),
                dma((n_steps,)),
                dma((n_steps, 2)),
                dma((n_steps, 2)),
            ],
            compiler_params=pltpu.CompilerParams(
                collective_id=0, has_side_effects=True, vmem_limit_bytes=67043328
            ),
        )(coeffs, ham_alpha, ham_beta)

    in_specs = (P("row", "col"), P("row", None), P("col", None))
    return jax.shard_map(
        local, mesh=mesh, in_specs=in_specs, out_specs=P("row", "col"), check_vma=False
    )
```

```python
import functools

import jax
import jax.numpy as jnp
from jax import lax
from jax.experimental import pallas as pl
from jax.experimental.pallas import tpu as pltpu
from jax.sharding import PartitionSpec as P

PAIR = 2
MESH = pl.DeviceIdType.MESH


def flip(index, key):
    bit = 1
    while bit <= key:
        if key & bit:
            index = index + bit - 2 * bit * ((index // bit) % 2)
        bit *= 2
    return index


def split(value):
    high = value.astype(jnp.bfloat16)
    return high, (value - high.astype(jnp.float32)).astype(jnp.bfloat16)


def product(lhs, rhs, rhs_dim):
    lhs_high, lhs_low = split(lhs)
    rhs_high, rhs_low = split(rhs)

    def one(a, b):
        return lax.dot_general(
            a, b, (((1,), (rhs_dim,)), ((), ())), preferred_element_type=jnp.float32
        )

    return one(lhs_high, rhs_high) + (one(lhs_high, rhs_low) + one(lhs_low, rhs_high))


def exchanges(n):
    held, mask, out = [0], n // 2, []
    while mask:
        out += [(mask, key) for key in held]
        held += [key ^ mask for key in held]
        mask //= 2
    return out


def kernel(
    line, cols_n, cw, width,
    coeffs, ha, hb, out,
    ham, beta, co, ag, sums, sums_in, acc, acc_in, turned, back_in,
    load_sem, ag_send, ag_recv, s_send, s_recv, o_send, o_recv,
    x_send, x_recv, p_send, p_recv, c_send, c_recv,
):
    rows, cols = coeffs.shape
    nk = cols // cw - 1
    row, col = lax.axis_index("row"), lax.axis_index("col")
    z, x = row // PAIR, row % PAIR
    partner = z * PAIR + 1 - x
    steps = exchanges(cols_n)
    masks = sorted({mask for mask, _ in steps}, reverse=True)

    def there(to_row, to_col):
        return (to_row, to_col)

    def ham_load(s):
        at = pl.multiple_of((s * PAIR + x) * rows, 128)
        return pltpu.make_async_copy(ha.at[:, pl.ds(at, rows)], ham.at[0, s], load_sem.at[s])

    def beta_load(key):
        at = pl.multiple_of(flip(col, key) * cols, 128)
        return pltpu.make_async_copy(
            hb.at[:, pl.ds(at, cols)], beta.at[key], load_sem.at[line + key]
        )

    beta_load(0).start()
    for s in range(line):
        ham_load(s).start()
    for key in range(1, cols_n):
        beta_load(key).start()

    barrier = pltpu.get_barrier_semaphore()
    has_low, has_high = z > 0, z < line - 1
    pl.semaphore_signal(barrier, inc=1, device_id=there(partner, col), device_id_type=MESH)
    for mask in masks:
        pl.semaphore_signal(
            barrier, inc=1, device_id=there(row, flip(col, mask)), device_id_type=MESH
        )

    @pl.when(has_low)
    def _():
        pl.semaphore_signal(barrier, inc=1, device_id=there(row - PAIR, col), device_id_type=MESH)

    @pl.when(has_high)
    def _():
        pl.semaphore_signal(barrier, inc=1, device_id=there(row + PAIR, col), device_id_type=MESH)

    inner = jnp.logical_and(has_low, has_high)

    @pl.when(inner)
    def _():
        pl.semaphore_wait(barrier, 3 + len(masks))

    @pl.when(jnp.logical_not(inner))
    def _():
        pl.semaphore_wait(barrier, 2 + len(masks))

    def remote(src, dst, send, recv, to):
        return pltpu.make_async_remote_copy(
            src_ref=src, dst_ref=dst, send_sem=send, recv_sem=recv,
            device_id=to, device_id_type=MESH,
        )

    def slot(index):
        first = index * width
        at = pl.multiple_of(first % rows, 128)
        return ham.at[1, first // rows, :, pl.ds(at, width)]

    def piece_copy():
        first = col * width
        at = pl.multiple_of((first // rows * PAIR + 1 - x) * rows + first % rows, 128)
        return remote(
            ha.at[:, pl.ds(at, width)], slot(col), x_send.at[0], x_recv.at[0], there(partner, col)
        )

    def back_copy():
        return remote(
            coeffs.at[:, pl.ds(nk * cw, cw)], back_in, x_send.at[1], x_recv.at[1],
            there(partner, col),
        )

    def other_copy(k):
        return remote(acc.at[1, k], acc_in.at[k], o_send.at[k], o_recv.at[k], there(partner, col))

    def ag_copy(d, t, k):
        src = coeffs.at[:, pl.ds(pl.multiple_of(k * cw, 128), cw)] if t == 1 else ag.at[d, t - 2, k]
        to = there(row + PAIR if d == 0 else row - PAIR, col)
        return remote(src, ag.at[d, t - 1, k], ag_send.at[d, t - 1, k], ag_recv.at[d, t - 1, k], to)

    def ag_sends(d, t):
        if d == 0:
            return jnp.logical_and(has_high, z >= t - 1)
        return jnp.logical_and(has_low, z <= line - t)

    def ag_gets(d, t):
        return z >= t if d == 0 else z <= line - 1 - t

    def s_copy(d, m):
        to = there(row + PAIR if d == 0 else row - PAIR, col)
        return remote(sums.at[d, m - 1], sums_in.at[d, m - 1], s_send.at[d, m - 1], s_recv.at[d, m - 1], to)

    def s_sends(d, m):
        return z <= line - 1 - m if d == 0 else z >= m

    def s_gets(d, m):
        if d == 0:
            return jnp.logical_and(z >= 1, z - 1 <= line - 1 - m)
        return jnp.logical_and(z <= line - 2, z + 1 >= m)

    def p_copy(i):
        mask, key = steps[i]
        place = slot(flip(col, key))
        return remote(place, place, p_send.at[i], p_recv.at[i], there(row, flip(col, mask)))

    def p_got(i):
        mask, key = steps[i]
        place = slot(flip(col, key ^ mask))
        return remote(place, place, p_send.at[i], p_recv.at[i], there(row, flip(col, mask)))

    half = rows // 2

    def c_copy(i, h):
        mask, key = steps[i]
        part = pl.ds(h * half, half)
        src = coeffs.at[part] if key == 0 else co.at[key - 1, part]
        return remote(
            src, co.at[(key ^ mask) - 1, part], c_send.at[i, h], c_recv.at[i, h],
            there(row, flip(col, mask)),
        )

    piece_copy().start()
    for d in range(2):
        @pl.when(ag_sends(d, 1))
        def _(d=d):
            for k in range(nk):
                ag_copy(d, 1, k).start()
    c_copy(0, 0).start()
    back_copy().start()

    tile = min(256, cols)

    def beta_tile(key_ref, beta_ref, n, add):
        at = pl.ds(pl.multiple_of(n * tile, 128), tile)
        value = product(key_ref[...], beta_ref[at, :], 1)
        out[:, at] = out[:, at] + value if add else value

    beta_load(0).wait()

    @pl.loop(0, cols // tile)
    def _(n):
        beta_tile(coeffs, beta.at[0], n, False)

    turned[0] = coeffs[:, nk * cw:].T
    for s in range(line):
        ham_load(s).wait()
    for key in range(1, cols_n):
        beta_load(key).wait()

    piece_copy().wait_recv()
    p_copy(0).start()
    c_copy(0, 1).start()

    def pass_on(t, ks):
        for k in ks:
            for d in range(2):
                @pl.when(ag_gets(d, t))
                def _(d=d, k=k):
                    ag_copy(d, t, k).wait_recv()

                if t + 1 < line:
                    @pl.when(ag_sends(d, t + 1))
                    def _(d=d, k=k):
                        ag_copy(d, t + 1, k).start()

    pass_on(1, range(nk))

    for mask in masks:
        group = [i for i, step in enumerate(steps) if step[0] == mask]
        for i in group:
            if i:
                p_copy(i).start()
        for i in group:
            p_got(i).wait_recv()
    back_copy().wait_recv()
    turned[1] = back_in[...].T

    def term(s):
        def body(m, total):
            return total + product(turned[m], ham[m, s], 0)

        return lax.fori_loop(0, PAIR, body, jnp.zeros((cw, rows), jnp.float32))

    def send_sums(m):
        for d in range(2):
            @pl.when(s_sends(d, m))
            def _(d=d):
                sums[d, m - 1] = term(z + m if d == 0 else z - m)

            if m + 1 < line:
                @pl.when(s_gets(d, m + 1))
                def _(d=d):
                    s_copy(d, m + 1).wait_recv()

                @pl.when(jnp.logical_and(s_gets(d, m + 1), s_sends(d, m)))
                def _(d=d):
                    sums[d, m - 1] = sums[d, m - 1] + sums_in[d, m]

            @pl.when(s_sends(d, m))
            def _(d=d):
                s_copy(d, m).start()

    def add_products(d, t, k):
        s = z - t if d == 0 else z + t

        @pl.loop(0, PAIR)
        def _(m):
            acc[m, k] = acc[m, k] + product(ham[m, s], ag[d, t - 1, k], 0)

    def add_step(t):
        for d in range(2):
            @pl.when(ag_gets(d, t))
            def _(d=d):
                @pl.loop(0, nk)
                def _(k):
                    add_products(d, t, k)

    early = line > 3
    if early:
        pass_on(2, range(min(1, nk)))
    send_sums(line - 1)
    if early:
        pass_on(2, range(1, nk - 1))

    @pl.loop(0, nk)
    def _(k):
        own = coeffs.at[:, pl.ds(pl.multiple_of(k * cw, 128), cw)]

        @pl.loop(0, PAIR)
        def _(m):
            acc[m, k] = product(ham[m, z], own[...], 0)

    def coeffs_step(mask):
        group = [i for i, step in enumerate(steps) if step[0] == mask]
        for i in group:
            if i:
                for h in range(2):
                    c_copy(i, h).start()
        for i in group:
            for h in range(2):
                c_copy(i, h).wait_recv()

    if early:
        pass_on(2, range(max(1, nk - 1), nk))
    for t in range(2, line):
        if 2 < t < line - 1:
            pass_on(t, range(nk))
        if t < line - 1:
            send_sums(line - t)
        if t == 2:
            coeffs_step(masks[0])
            if len(masks) > 1:
                for i, step in enumerate(steps):
                    if step[0] == masks[1]:
                        for h in range(2):
                            c_copy(i, h).start()
        add_step(t - 1)

    def coeffs_rest():
        for j, mask in enumerate(masks):
            group = [i for i, step in enumerate(steps) if step[0] == mask]
            if j >= 2:
                for i in group:
                    for h in range(2):
                        c_copy(i, h).start()
            if j >= 1:
                for i in group:
                    for h in range(2):
                        c_copy(i, h).wait_recv()

    def add_beta(key):
        @pl.loop(0, cols // tile)
        def _(n):
            beta_tile(co.at[key - 1], beta.at[key], n, True)

    t = line - 1
    for k in range(nk):
        for d in range(2):
            @pl.when(ag_gets(d, t))
            def _(d=d, k=k):
                ag_copy(d, t, k).wait_recv()
                add_products(d, t, k)

        other_copy(k).start()
        if k == 0:
            send_sums(1)
            coeffs_rest()
        if k + 1 < cols_n:
            add_beta(k + 1)

    @pl.loop(nk + 1, cols_n)
    def _(key):
        add_beta(key)

    tail = term(z)
    for d in range(2):
        @pl.when(s_gets(d, 1))
        def _(d=d):
            s_copy(d, 1).wait_recv()
    sums[0, line - 1] = tail
    for d in range(2):
        @pl.when(s_gets(d, 1))
        def _(d=d):
            sums[0, line - 1] = sums[0, line - 1] + sums_in[d, 0]
    out[:, nk * cw:] = out[:, nk * cw:] + sums[0, line - 1].T

    @pl.loop(0, nk)
    def _(k):
        at = pl.ds(pl.multiple_of(k * cw, 128), cw)
        other_copy(k).wait_recv()
        out[:, at] = out[:, at] + (acc[0, k] + acc_in[k])

    piece_copy().wait_send()
    back_copy().wait_send()
    for i in range(len(steps)):
        p_copy(i).wait_send()
        for h in range(2):
            c_copy(i, h).wait_send()
    for d in range(2):
        for m in range(1, line):
            @pl.when(ag_sends(d, m))
            def _(d=d, m=m):
                for k in range(nk):
                    ag_copy(d, m, k).wait_send()

            @pl.when(s_sends(d, m))
            def _(d=d, m=m):
                s_copy(d, m).wait_send()

    @pl.loop(0, nk)
    def _(k):
        other_copy(k).wait_send()


def solution(mesh):
    line, cols_n = mesh.shape["row"] // PAIR, mesh.shape["col"]
    n_steps = len(exchanges(cols_n))

    def local(coeffs, ham_alpha, ham_beta):
        rows, cols = coeffs.shape
        cw = min(256, cols // 2)
        nk = cols // cw - 1
        width = line * rows // cols_n
        f32, dma = jnp.float32, pltpu.SemaphoreType.DMA
        any_spec = pl.BlockSpec(memory_space=pl.ANY)
        vmem_spec = pl.BlockSpec(memory_space=pltpu.VMEM)
        return pl.pallas_call(
            functools.partial(kernel, line, cols_n, cw, width),
            out_shape=jax.ShapeDtypeStruct((rows, cols), f32),
            in_specs=[vmem_spec, any_spec, any_spec],
            out_specs=vmem_spec,
            scratch_shapes=[
                pltpu.VMEM((PAIR, line, rows, rows), f32),
                pltpu.VMEM((cols_n, cols, cols), f32),
                pltpu.VMEM((cols_n - 1, rows, cols), f32),
                pltpu.VMEM((2, line - 1, nk, rows, cw), f32),
                pltpu.VMEM((2, line, cw, rows), f32),
                pltpu.VMEM((2, line - 1, cw, rows), f32),
                pltpu.VMEM((PAIR, nk, rows, cw), f32),
                pltpu.VMEM((nk, rows, cw), f32),
                pltpu.VMEM((PAIR, cw, rows), f32),
                pltpu.VMEM((rows, cw), f32),
                dma((line + cols_n,)),
                dma((2, line - 1, nk)),
                dma((2, line - 1, nk)),
                dma((2, line - 1)),
                dma((2, line - 1)),
                dma((nk,)),
                dma((nk,)),
                dma((2,)),
                dma((2,)),
                dma((n_steps,)),
                dma((n_steps,)),
                dma((n_steps, 2)),
                dma((n_steps, 2)),
            ],
            compiler_params=pltpu.CompilerParams(
                collective_id=0, has_side_effects=True, vmem_limit_bytes=67043328
            ),
        )(coeffs, ham_alpha, ham_beta)

    in_specs = (P("row", "col"), P("row", None), P("col", None))
    return jax.shard_map(
        local, mesh=mesh, in_specs=in_specs, out_specs=P("row", "col"), check_vma=False
    )
```
